128 devices in a mesh: pos: 16 (over x, z), tile: 8 (over y, core).
Axes of the slice: x: 4, y: 4, z: 4, core: 2. Of those that a mesh axis runs over, the one named last changes fastest.
Arguments:
- probe_modes: float32 [8, 2, 256, 256], P('tile'), may hold values from -1.1 to 1.1
- object_slices: bfloat16 [2, 2, 512, 2048], P(None, None, 'tile'), may hold values from -6 to 6
- amplitudes: bfloat16 [128, 256, 256], P('pos'), may hold values from 0.5 to 3
- scan_offsets: int32 [128, 2], replicated, may hold values from 0 to 1792, as said below
- slot_counts: int32 [16], replicated, may hold values from 1 to 8, 64 in all
Outputs:
- object_grad: float32 [2, 2, 512, 2048], P(None, None, 'tile', 'pos')
- probe_grad: float32 [8, 2, 256, 256], P('tile', None, 'pos')
The draws below stay inside these ranges and needn't reach their ends.
Inputs may be any that keep to these rules, and one draw needn't show every extreme that they name: slot_counts[g] is how many leading slots of group g are live scan positions; the counts sum to 64 and the largest is exactly 8. scan_offsets[s] is (row, column); the row is at most 256 and the column at most 1792, both reached in every draw.
All inputs are finite; a program needn't handle non-finite values.
Results may differ from the reference program's by a relative error of at most 0.025.
Values may be sent and summed in bfloat16 or wider, within the bound.
A program may use at most 128 MiB of HBM per device.

```python
import math
import jax
import jax.numpy as jnp
import numpy as np
from jax import lax

SIDE = 256
MODES = 8
LAYERS = 2
ROWS = 512
COLS = 2048
SLOTS = 8
GROUPS = 16
SLOT_ALL = 128
POSITIONS = 64


def draw_scan_offsets(key, part):
    first_key, second_key = jax.random.split(key)
    row_list = jax.random.randint(first_key, (SLOT_ALL,), 0, ROWS - SIDE + 1, dtype=jnp.int32)
    col_list = jax.random.randint(second_key, (SLOT_ALL,), 0, COLS - SIDE + 1, dtype=jnp.int32)
    row_list = row_list.at[1].set(ROWS - SIDE)
    col_list = col_list.at[0].set(COLS - SIDE)
    return jnp.stack([row_list, col_list], axis=1).astype(jnp.int32)


def level_of(key, shape, cuts, smallest, top_value):
    def one(position, blocks):
        draws = jax.random.uniform(jax.random.fold_in(jax.random.fold_in(key, 6), position), (blocks,), jnp.float32, smallest / len(cuts), top_value / len(cuts))
        return jnp.repeat(jnp.exp(draws), shape[position] // blocks).reshape((-1,) + (1,) * (len(shape) - position - 1))

    level = one(*cuts[0])
    for cut in cuts[1:]:
        level = level * one(*cut)
    return level


def length_profile(amount, total, most, lean):
    weights = [(1 << 20) // math.isqrt(standing ** lean) + 1 for standing in range(2, amount + 1)]
    surplus, counts = total - most - (amount - 1), [1] * (amount - 1)
    while surplus > 0:
        free = [i for i in range(amount - 1) if counts[i] < most]
        mass, left = sum([weights[i] for i in free]), surplus
        for i in free:
            more = min(most - counts[i], max(1, left * weights[i] // mass), surplus)
            counts[i] = counts[i] + more
            surplus = surplus - more
    return np.array([most] + counts)


def uneven_parts(stream_key, count, total, most, skew):
    if count == 2:
        one = jax.random.randint(stream_key, (), max(1, total - most), min(most, total - 1) + 1)
        return jnp.stack([one, total - one])
    sizes = jnp.asarray(length_profile(count, total, most, skew), jnp.int32)
    couples = (count - 1) // 2
    giver, taker = sizes[1:1 + 2 * couples:2], sizes[2:2 + 2 * couples:2]
    room = jnp.minimum(giver - 1, most - taker)
    moved = jax.random.randint(jax.random.fold_in(stream_key, 1), (couples,), 0, 1 << 20) % (room + 1)
    sizes = sizes.at[1:1 + 2 * couples:2].set(giver - moved).at[2:2 + 2 * couples:2].set(taker + moved)
    return sizes[jax.random.permutation(jax.random.fold_in(stream_key, 2), count)]


def bell_draw(stream_key, dims, deviation, most, shards=(), kind=jnp.bfloat16):
    values = deviation * jax.random.normal(stream_key, dims, jnp.float32)
    if shards:
        values = values * level_of(stream_key, dims, shards, -0.22, 0.18)
    return jnp.clip(values, -most, most).astype(kind)


def setup_inputs(seed: int = 0) -> dict:
    keys = jax.random.split(jax.random.key(seed), 6)
    return {
        "probe_modes": bell_draw(keys[0], (MODES, 2, SIDE, SIDE), 0.18, 1.1, ((0, 8),), jnp.float32),
        "object_slices": bell_draw(keys[1], (LAYERS, 2, ROWS, COLS), 1.0, 6.0, ((2, 8),)),
        "amplitudes": jnp.clip(0.5 + 2.5 * jax.random.uniform(keys[2], (SLOT_ALL, SIDE, SIDE), jnp.float32) ** level_of(keys[2], (SLOT_ALL, SIDE, SIDE), ((0, 16),), -0.2, 0.2), 0.5, 3.0).astype(jnp.bfloat16),
        "scan_offsets": draw_scan_offsets(jax.random.fold_in(keys[5], 71), 0),
        "slot_counts": uneven_parts(keys[4], GROUPS, POSITIONS, SLOTS, 2).astype(jnp.int32),
    }


FRESNEL = 0.37

def make_tables(points):
    counter = jnp.arange(points, dtype=jnp.int32)
    product = counter[:, None] * counter[None, :] % points
    angle = 2.0 * jnp.pi / points * product.astype(jnp.float32)
    factor = 1.0 / jnp.sqrt(jnp.float32(points))
    table_re = (jnp.cos(angle) * factor).astype(jnp.bfloat16)
    table_im = (-jnp.sin(angle) * factor).astype(jnp.bfloat16)
    shifted = ((counter + points // 2) % points - points // 2).astype(jnp.float32)
    phase = jnp.pi * FRESNEL / points * (shifted[:, None] * shifted[:, None] + shifted[None, :] * shifted[None, :])
    kernel = jnp.stack([jnp.cos(phase), -jnp.sin(phase)])
    return (table_re, table_im, kernel)

def times_complex(first, second):
    real_part = first[..., 0, :, :] * second[..., 0, :, :] - first[..., 1, :, :] * second[..., 1, :, :]
    imag_part = first[..., 0, :, :] * second[..., 1, :, :] + first[..., 1, :, :] * second[..., 0, :, :]
    return jnp.stack([real_part, imag_part], axis=-3)

def conjugate(values):
    return jnp.stack([values[..., 0, :, :], -values[..., 1, :, :]], axis=-3)

def transform_one(values, table_re, table_im):
    points = table_re.shape[0]
    lowered = values.astype(jnp.bfloat16)
    left_side = jnp.concatenate([table_re, table_im], axis=0)
    right_side = jnp.concatenate([lowered[0], lowered[1]], axis=1)
    first = jnp.dot(left_side, right_side, preferred_element_type=jnp.float32)
    mid_re = (first[:points, :points] - first[points:, points:]).astype(jnp.bfloat16)
    mid_im = (first[:points, points:] + first[points:, :points]).astype(jnp.bfloat16)
    second = jnp.dot(jnp.concatenate([mid_re, mid_im], axis=0), jnp.concatenate([table_re, table_im], axis=1), preferred_element_type=jnp.float32)
    out_re = second[:points, :points] - second[points:, points:]
    out_im = second[:points, points:] + second[points:, :points]
    return jnp.stack([out_re, out_im])

def propagate_one(values, table_re, table_im, kernel):
    return transform_one(times_complex(transform_one(values, table_re, table_im), kernel), table_re, -table_im)

def slot_terms(probe_modes, window, amplitude, table_re, table_im, kernel):
    layers = window.shape[0]
    kernel_conj = conjugate(kernel)

    def forward(mode_probe):
        current = times_complex(mode_probe, window[0])
        entering = []
        for layer_at in range(1, layers):
            arrived = propagate_one(current, table_re, table_im, kernel)
            entering.append(arrived)
            current = times_complex(arrived, window[layer_at])
        return (jnp.stack(entering), transform_one(current, table_re, table_im))
    entering, far_field = lax.map(forward, probe_modes)
    power = lax.optimization_barrier(jnp.sum(far_field * far_field, axis=(0, 1)))
    ratio = 1.0 - amplitude / jnp.sqrt(power + 1.0)

    def backward(packed):
        mode_probe, arrived_all, far_one = packed
        incoming = transform_one(ratio * far_one, table_re, -table_im)
        grads = [None] * layers
        for layer_at in range(layers - 1, 0, -1):
            grads[layer_at] = times_complex(conjugate(arrived_all[layer_at - 1]), incoming)
            incoming = propagate_one(times_complex(conjugate(window[layer_at]), incoming), table_re, table_im, kernel_conj)
        grads[0] = times_complex(conjugate(mode_probe), incoming)
        probe_term = times_complex(conjugate(window[0]), incoming)
        return (jnp.stack(grads), probe_term)
    object_terms, probe_terms = lax.map(backward, (probe_modes, entering, far_field))
    return (lax.optimization_barrier(jnp.sum(object_terms, axis=0)), probe_terms)

def window_anchor(place):
    zero_index = jnp.int32(0)
    return (zero_index, zero_index, place[0].astype(jnp.int32), place[1].astype(jnp.int32))

def reference(probe_modes, object_slices, amplitudes, scan_offsets, slot_counts):
    points = probe_modes.shape[-1]
    layers = object_slices.shape[0]
    table_re, table_im, kernel = make_tables(points)
    live = (jnp.arange(SLOTS, dtype=jnp.int32)[None, :] < slot_counts[:, None].astype(jnp.int32)).reshape(-1)
    canvas = jnp.zeros(object_slices.shape, jnp.float32)
    probe_sum = jnp.zeros(probe_modes.shape, jnp.float32)

    def step(carry, packed):
        canvas, probe_sum = carry
        place, amplitude, alive = packed
        anchor = window_anchor(place)
        window = lax.dynamic_slice(object_slices, anchor, (layers, 2, points, points)).astype(jnp.float32)

        def active(unused):
            return slot_terms(probe_modes, window, amplitude, table_re, table_im, kernel)

        def inactive(unused):
            return (jnp.zeros((layers, 2, points, points), jnp.float32), jnp.zeros(probe_modes.shape, jnp.float32))
        object_term, probe_term = lax.cond(alive, active, inactive, 0)
        current = lax.dynamic_slice(canvas, anchor, (layers, 2, points, points))
        canvas = lax.dynamic_update_slice(canvas, current + object_term, anchor)
        return ((canvas, probe_sum + probe_term), None)
    (canvas, probe_sum), unused = lax.scan(step, (canvas, probe_sum), (scan_offsets.astype(jnp.int32), amplitudes.astype(jnp.float32), live))
    return (canvas, probe_sum)
```

```python
import functools

import jax
import jax.numpy as jnp
import numpy as np
from jax import lax
from jax.experimental import pallas as pl
from jax.experimental.pallas import tpu as pltpu
from jax.sharding import PartitionSpec as P

FRESNEL = 0.37
LINE = 4
F32 = jnp.float32
BF16 = jnp.bfloat16
MESH = pl.DeviceIdType.MESH


def tables(points):
    counter = np.arange(points, dtype=np.int32)
    product = counter[:, None] * counter[None, :] % points
    angle = np.float32(2.0 * np.pi / points) * product.astype(np.float32)
    factor = np.float32(1.0) / np.sqrt(np.float32(points))
    re = (np.cos(angle) * factor).astype(np.float32)
    im = (-np.sin(angle) * factor).astype(np.float32)
    a = np.block([[re, -im], [im, re]]).astype(jnp.bfloat16)
    b = np.block([[re, im], [-im, re]]).astype(jnp.bfloat16)
    shifted = ((counter + points // 2) % points - points // 2).astype(np.float32)
    phase = np.float32(np.pi * FRESNEL / points) * (shifted[:, None] ** 2 + shifted[None, :] ** 2)
    ker = np.stack([np.cos(phase), -np.sin(phase)]).astype(np.float32)
    return a, b, ker


def one_hot(shape, shift, transposed=False):
    rows = lax.broadcasted_iota(jnp.int32, shape, 0)
    cols = lax.broadcasted_iota(jnp.int32, shape, 1)
    hit = (cols == rows + shift) if transposed else (rows == cols + shift)
    return jnp.where(hit, 1.0, 0.0).astype(BF16)


def dot(left, right):
    return jnp.dot(left, right, preferred_element_type=F32)


def body(
    counts, offs, probe, strip, amp, amat, bmat, ker, obj_out, prb_out,
    tall, wsend, wbuf, win, prb, asend, arecv, ahalf, phi, far, pwsend, pwrecv, ratio, xin,
    g1, g0, sibs, sibr, own, gys, gyr, pad, canvas, posr, gps, gpr, gsum, gfr,
    w_ss, w_rs, rl_ss, rl_rs, p_ss, p_rs, a_ss, a_rs, ah_ss, ah_rs, pw_ss, pw_rs,
    sb_ss, sb_rs, gy_ss, gy_rs, ps_ss, ps_rs, gp_ss, gp_rs, gf_ss, gf_rs,
    *, n_pos,
):
    p = lax.axis_index("pos")
    t = lax.axis_index("tile")
    y = lax.div(t, 2)
    c = lax.rem(t, 2)
    S = ker.shape[1]
    H = S // 2
    layers, _, SR, C = strip.shape
    CW = C // n_pos
    slots = amp.shape[0]
    groups = counts.shape[0]
    RW = SR * 2 * LINE

    def at_y(i):
        return lax.rem(y + i, LINE)

    def ydev(i):
        return (p, 2 * at_y(i) + c)

    sib = (p, 2 * y + 1 - c)

    def pdev(d):
        return (lax.rem(p + d, n_pos), t)

    def copy(src, dst, ss, rs, dev):
        return pltpu.make_async_remote_copy(
            src_ref=src, dst_ref=dst, send_sem=ss, recv_sem=rs, device_id=dev, device_id_type=MESH
        )

    barrier = pltpu.get_barrier_semaphore()
    partners = [ydev(i) for i in range(1, LINE)] + [sib] + [pdev(d) for d in range(1, n_pos)]
    for dev in partners:
        pl.semaphore_signal(barrier, inc=1, device_id=dev, device_id_type=MESH)

    def locate(k):
        g = jnp.int32(0)
        start = jnp.int32(0)
        end = jnp.int32(0)
        for q in range(groups):
            end = end + counts[q]
            past = end <= k
            g = jnp.where(past, q + 1, g)
            start = jnp.where(past, end, start)
        return jnp.clip(slots * g + (k - start), 0, slots * groups - 1)

    row_of, base_of, shift_of = [], [], []
    for i in range(LINE):
        s = locate(LINE * p + at_y(i))
        row_of.append(offs[s, 0])
        col = offs[s, 1]
        block = jnp.int32(0)
        for q in range(1, (C - S) // 128):
            block = jnp.where(col >= q * 128, q, block)
        base_of.append(block)
        shift_of.append(col - block * 128)
    wide = S + 128
    my_row = row_of[0]

    my_start = jnp.int32(0)
    for q in range(groups):
        my_start = my_start + jnp.where(q < p, counts[q], 0)
    my_count = counts[p]

    def crop(l):
        for q in range(C // 128):
            tall[l, q] = strip[l, :, :, q * 128 : (q + 1) * 128].reshape(2 * SR, 128)
        for i in range(LINE):
            sel = one_hot((wide, S), shift_of[i])
            blk = jnp.concatenate([tall[l, base_of[i] + q] for q in range(wide // 128)], axis=-1)
            out = dot(blk, sel).astype(BF16).reshape(2, SR, S)
            if i == 0:
                wbuf[l, :, pl.ds(pl.multiple_of(t * SR, SR), SR), :] = out
            else:
                wsend[l, i] = out

    def strip_rows(i):
        return pl.ds(pl.multiple_of((2 * at_y(i) + c) * SR, SR), SR)

    def w_copy(l, i):
        mine = pl.ds(pl.multiple_of(t * SR, SR), SR)
        return copy(wsend.at[l, i], wbuf.at[l, :, mine, :], w_ss.at[l, i], w_rs.at[l, i], ydev(i))

    def relay(l, i):
        ref = wbuf.at[l, :, strip_rows(LINE - i), :]
        return copy(ref, ref, rl_ss.at[l, i], rl_rs.at[l, i], sib)

    def p_copy(i):
        return copy(prb.at[0], prb.at[i], p_ss.at[i], p_rs.at[i], ydev(LINE - i))

    def a_copy(d):
        return copy(asend.at[d], arecv.at[d], a_ss.at[d], a_rs.at[d], pdev(d))

    near = (1, 3, 2)
    prb[0] = probe[0].astype(BF16)
    crop(0)
    pl.semaphore_wait(barrier, len(partners))
    for i in near:
        w_copy(0, i).start()
    relay(0, 0).start()
    for i in near:
        p_copy(i).start()
    crop(1)
    for i in near:
        w_copy(1, i).start()
    relay(1, 0).start()

    rows_c = pl.ds(pl.multiple_of(c * H, H), H)
    for d in range(n_pos):
        j = LINE * lax.rem(p + d, n_pos) + y - my_start
        keep = jnp.where((j >= 0) & (j < my_count), 1.0, 0.0)
        block = amp[jnp.clip(j, 0, slots - 1), rows_c, :].astype(F32) * keep
        if d == 0:
            arecv[0] = block.astype(BF16)
        else:
            asend[d] = block.astype(BF16)
    for d in range(1, n_pos):
        a_copy(d).start()

    def gather(l):
        for i in near:
            w_copy(l, i).wait_recv()
            relay(l, i).start()
        for i in range(LINE):
            relay(l, i).wait_recv()
        sel = one_hot((S, RW), my_row, transposed=True)
        win[l, 0] = dot(sel, wbuf[l, 0])
        win[l, 1] = dot(sel, wbuf[l, 1])

    def transform(re, im, left, right):
        x = jnp.concatenate([re.astype(BF16), im.astype(BF16)], axis=0)
        return transform_low(x, left, right)

    def transform_low(x, left, right):
        mid = dot(left[...], x).astype(BF16)
        out = dot(jnp.concatenate([mid[:S], mid[S:]], axis=1), right[...])
        return out[:, :S], out[:, S:]

    def forward_a(i):
        pr, pi = prb[i, 0].astype(F32), prb[i, 1].astype(F32)
        wr, wi = win[0, 0], win[0, 1]
        fr, fi = transform(pr * wr - pi * wi, pr * wi + pi * wr, amat, bmat)
        kr, ki = ker[0], ker[1]
        fr, fi = transform(fr * kr - fi * ki, fr * ki + fi * kr, bmat, amat)
        phi[i, 0] = fr
        phi[i, 1] = fi

    def forward_b(i):
        pr, pi = phi[i, 0], phi[i, 1]
        wr, wi = win[1, 0], win[1, 1]
        fr, fi = transform(pr * wr - pi * wi, pr * wi + pi * wr, amat, bmat)
        far[i, 0] = fr
        far[i, 1] = fi
        return fr * fr + fi * fi

    gather(0)
    forward_a(0)
    gather(1)
    ratio[...] = forward_b(0)
    for i in near:
        p_copy(i).wait_recv()
        forward_a(i)
        ratio[...] = ratio[...] + forward_b(i)

    pw_c = copy(pwsend, pwrecv, pw_ss.at[0], pw_rs.at[0], sib)
    pwsend[...] = ratio[...].astype(BF16)
    pw_c.start()
    total = arecv[0].astype(F32)
    for d in range(1, n_pos):
        a_copy(d).wait_recv()
        total = total + arecv[d].astype(F32)
    ahalf[rows_c, :] = total.astype(BF16)
    ah_c = copy(ahalf.at[rows_c, :], ahalf.at[rows_c, :], ah_ss.at[0], ah_rs.at[0], sib)
    ah_c.start()
    pw_c.wait_recv()
    power = ratio[...] + pwrecv[...].astype(F32)
    ah_c.wait_recv()
    ratio[...] = 1.0 - ahalf[...].astype(F32) / jnp.sqrt(power + 1.0)

    def backward_a(i, first):
        r = ratio[...]
        br, bi = transform(r * far[i, 0], r * far[i, 1], bmat, amat)
        pr, pi = phi[i, 0], phi[i, 1]
        gr = pr * br + pi * bi
        gi = pr * bi - pi * br
        if first:
            g1[0] = gr
            g1[1] = gi
        else:
            g1[0] = g1[0] + gr
            g1[1] = g1[1] + gi
        wr, wi = win[1, 0], win[1, 1]
        xin[i, :S] = (wr * br + wi * bi).astype(BF16)
        xin[i, S:] = (wr * bi - wi * br).astype(BF16)

    def backward_b(i, first):
        fr, fi = transform_low(xin[i], amat, bmat)
        kr, ki = ker[0], ker[1]
        br, bi = transform(fr * kr + fi * ki, fi * kr - fr * ki, bmat, amat)
        pr, pi = prb[i, 0].astype(F32), prb[i, 1].astype(F32)
        gr = pr * br + pi * bi
        gi = pr * bi - pi * br
        if first:
            g0[0] = gr
            g0[1] = gi
        else:
            g0[0] = g0[0] + gr
            g0[1] = g0[1] + gi
        wr, wi = win[0, 0], win[0, 1]
        gps[i, 0] = (wr * br + wi * bi).astype(BF16)
        gps[i, 1] = (wr * bi - wi * br).astype(BF16)

    def sb_copy(l):
        return copy(sibs.at[l], sibr.at[l], sb_ss.at[l], sb_rs.at[l], sib)

    def gy_copy(l, i):
        return copy(gys.at[l, i], gyr.at[l, i], gy_ss.at[l, i], gy_rs.at[l, i], ydev(i))

    def ps_copy(l, d):
        return copy(canvas.at[l, lax.rem(p + d, n_pos)], posr.at[l, d], ps_ss.at[l, d], ps_rs.at[l, d], pdev(d))

    def place_rows(l, grad):
        rows = lax.broadcasted_iota(jnp.int32, (RW, S), 0)
        cols = lax.broadcasted_iota(jnp.int32, (RW, S), 1)
        block = rows // SR
        strip_at = 2 * ((y + block % LINE) % LINE) + jnp.where(block < LINE, c, 1 - c)
        hit = strip_at * SR + rows % SR == cols + my_row
        sel = jnp.where(hit, 1.0, 0.0).astype(BF16)
        for part in range(2):
            out = dot(sel, grad[part].astype(BF16)).astype(BF16)
            for i in range(LINE):
                own[l, i, part] = out[i * SR : (i + 1) * SR]
                sibs[l, i, part] = out[(LINE + i) * SR : (LINE + i + 1) * SR]
        sb_copy(l).start()

    def add_cores(l):
        sb_copy(l).wait_recv()
        for i in (0, 2, 1, 3):
            both = (own[l, i].astype(F32) + sibr[l, i].astype(F32)).astype(BF16)
            if i == 0:
                gyr[l, 0] = both
            else:
                gys[l, i] = both
                gy_copy(l, i).start()

    def place_columns(l):
        for i in range(LINE):
            if i:
                gy_copy(l, i).wait_recv()
            k = (LINE - i) % LINE
            sel = one_hot((S, wide), shift_of[k], transposed=True)
            out = dot(gyr[l, i].reshape(2 * SR, S), sel).astype(BF16)
            for q in range(wide // 128):
                pad[l, i, q + 1] = out[:, q * 128 : (q + 1) * 128].reshape(2, SR, 128)
        per = CW // 128
        for q in range(C // 128):
            total = None
            for i in range(LINE):
                k = (LINE - i) % LINE
                at = jnp.clip(q - base_of[k], -1, wide // 128) + 1
                term = pad[l, i, at].astype(F32)
                total = term if total is None else total + term
            canvas[l, q // per, :, :, (q % per) * 128 : (q % per + 1) * 128] = total.astype(BF16)
        for d in range(1, n_pos):
            ps_copy(l, d).start()

    def finish(l):
        total = canvas[l, p].astype(F32)
        for d in range(1, n_pos):
            ps_copy(l, d).wait_recv()
            total = total + posr[l, d].astype(F32)
        obj_out[l] = total

    def gp_copy(i):
        return copy(gps.at[i], gpr.at[i], gp_ss.at[i], gp_rs.at[i], ydev(i))

    PR = S // n_pos

    def gf_copy(d):
        rows = pl.ds(pl.multiple_of(lax.rem(p + d, n_pos) * PR, PR), PR)
        return copy(gsum.at[:, rows, :], gfr.at[d], gf_ss.at[d], gf_rs.at[d], pdev(d))

    for n, i in enumerate((2, 1, 3, 0)):
        backward_a(i, n == 0)
    place_rows(1, g1)
    for l in range(layers):
        for i in range(LINE):
            pad[l, i, 0] = jnp.zeros((2, SR, 128), BF16)
            pad[l, i, wide // 128 + 1] = jnp.zeros((2, SR, 128), BF16)
    for n, i in enumerate((2, 1, 3, 0)):
        backward_b(i, n == 0)
        if i:
            gp_copy(i).start()
        if n == 0:
            add_cores(1)
        if n == 2:
            place_columns(1)
    place_rows(0, g0)
    gp_copy(1).wait_recv()
    gp_copy(3).wait_recv()
    gp_copy(2).wait_recv()
    for part in range(2):
        total = gps[0, part].astype(F32)
        for i in range(1, LINE):
            total = total + gpr[i, part].astype(F32)
        gsum[part] = total.astype(BF16)
    for d in range(1, n_pos):
        gf_copy(d).start()
    add_cores(0)
    place_columns(0)
    finish(1)
    my_rows = pl.ds(pl.multiple_of(p * PR, PR), PR)
    total = gsum[:, my_rows, :].astype(F32)
    for d in range(1, n_pos):
        gf_copy(d).wait_recv()
        total = total + gfr[d].astype(F32)
    prb_out[0] = total
    finish(0)

    for i in range(1, LINE):
        p_copy(i).wait_send()
        gp_copy(i).wait_send()
        for l in range(layers):
            w_copy(l, i).wait_send()
            gy_copy(l, i).wait_send()
    for l in range(layers):
        sb_copy(l).wait_send()
        for i in range(LINE):
            relay(l, i).wait_send()
        for d in range(1, n_pos):
            ps_copy(l, d).wait_send()
    for d in range(1, n_pos):
        a_copy(d).wait_send()
        gf_copy(d).wait_send()
    pw_c.wait_send()
    ah_c.wait_send()


def on_device(n_pos, consts, probe_modes, object_slices, amplitudes, scan_offsets, slot_counts):
    S = probe_modes.shape[-1]
    layers, _, SR, C = object_slices.shape
    CW = C // n_pos
    RW = SR * 2 * LINE
    wide = S + 128
    vm = pltpu.VMEM
    dma = pltpu.SemaphoreType.DMA
    scratch = [
        vm((layers, C // 128, 2 * SR, 128), BF16),
        vm((layers, LINE, 2, SR, S), BF16),
        vm((layers, 2, RW, S), BF16),
        vm((layers, 2, S, S), F32),
        vm((LINE, 2, S, S), BF16),
        vm((n_pos, S // 2, S), BF16),
        vm((n_pos, S // 2, S), BF16),
        vm((S, S), BF16),
        vm((LINE, 2, S, S), F32),
        vm((LINE, 2, S, S), F32),
        vm((S, S), BF16),
        vm((S, S), BF16),
        vm((S, S), F32),
        vm((LINE, 2 * S, S), BF16),
        vm((2, S, S), F32),
        vm((2, S, S), F32),
        vm((layers, LINE, 2, SR, S), BF16),
        vm((layers, LINE, 2, SR, S), BF16),
        vm((layers, LINE, 2, SR, S), BF16),
        vm((layers, LINE, 2, SR, S), BF16),
        vm((layers, LINE, 2, SR, S), BF16),
        vm((layers, LINE, wide // 128 + 2, 2, SR, 128), BF16),
        vm((layers, n_pos, 2, SR, CW), BF16),
        vm((layers, n_pos, 2, SR, CW), BF16),
        vm((LINE, 2, S, S), BF16),
        vm((LINE, 2, S, S), BF16),
        vm((2, S, S), BF16),
        vm((n_pos, 2, S // n_pos, S), BF16),
    ]
    for shape in (
        (layers, LINE), (layers, LINE), (LINE,), (n_pos,), (1,), (1,),
        (layers,), (layers, LINE), (layers, n_pos), (LINE,), (n_pos,),
    ):
        scratch += [dma(shape), dma(shape)]
    smem = pl.BlockSpec(memory_space=pltpu.SMEM)
    vmem = pl.BlockSpec(memory_space=pltpu.VMEM)
    return pl.pallas_call(
        functools.partial(body, n_pos=n_pos),
        out_shape=(
            jax.ShapeDtypeStruct((layers, 2, SR, CW), F32),
            jax.ShapeDtypeStruct((1, 2, S // n_pos, S), F32),
        ),
        in_specs=[smem, smem] + [vmem] * 6,
        out_specs=(vmem, vmem),
        scratch_shapes=scratch,
        compiler_params=pltpu.CompilerParams(
            collective_id=0, has_side_effects=True, vmem_limit_bytes=60 * 1024 * 1024
        ),
        name="ptycho",
    )(slot_counts, scan_offsets, probe_modes, object_slices, amplitudes, *consts)


def solution(mesh):
    n_pos = mesh.shape["pos"]
    in_specs = (
        P("tile", None, None, None),
        P(None, None, "tile", None),
        P("pos", None, None),
        P(),
        P(),
    )
    out_specs = (P(None, None, "tile", "pos"), P("tile", None, "pos", None))

    def run(probe_modes, object_slices, amplitudes, scan_offsets, slot_counts):
        consts = tuple(jnp.asarray(v) for v in tables(probe_modes.shape[-1]))
        return jax.shard_map(
            lambda *args: on_device(n_pos, args[5:], *args[:5]),
            mesh=mesh,
            in_specs=in_specs + (P(), P(), P()),
            out_specs=out_specs,
            check_vma=False,
        )(probe_modes, object_slices, amplitudes, scan_offsets, slot_counts, *consts)

    return run
```

```python
import functools
import math

import jax
import jax.numpy as jnp
import numpy as np
from jax import lax
from jax.experimental import pallas as pl
from jax.experimental.pallas import tpu as pltpu
from jax.sharding import PartitionSpec as P

FRESNEL = 0.37
LINE = 4
F32 = jnp.float32
BF16 = jnp.bfloat16
MESH = pl.DeviceIdType.MESH


def tables(points):
    counter = np.arange(points, dtype=np.int32)
    product = counter[:, None] * counter[None, :] % points
    angle = np.float32(2.0 * np.pi / points) * product.astype(np.float32)
    factor = np.float32(1.0) / np.sqrt(np.float32(points))
    re = (np.cos(angle) * factor).astype(np.float32)
    im = (-np.sin(angle) * factor).astype(np.float32)
    a = np.block([[re, -im], [im, re]]).astype(jnp.bfloat16)
    b = np.block([[re, im], [-im, re]]).astype(jnp.bfloat16)
    shifted = ((counter + points // 2) % points - points // 2).astype(np.float32)
    phase = np.float32(np.pi * FRESNEL / points) * (shifted[:, None] ** 2 + shifted[None, :] ** 2)
    ker = np.stack([np.cos(phase), -np.sin(phase)]).astype(np.float32)
    return a, b, ker


def one_hot(shape, shift, transposed=False):
    rows = lax.broadcasted_iota(jnp.int32, shape, 0)
    cols = lax.broadcasted_iota(jnp.int32, shape, 1)
    hit = (cols == rows + shift) if transposed else (rows == cols + shift)
    return jnp.where(hit, 1.0, 0.0).astype(BF16)


def dot(left, right):
    return jnp.dot(left, right, preferred_element_type=F32)


def body(
    counts, offs, probe_in, strip_in, amp_in, amat_in, bmat_in, ker_in, obj_out, prb_out,
    probe, strip, amp, amat, bmat, ker,
    tall, wsend, wbuf, win, prb, asend, arecv, ahalf, phi, far, pwsend, pwrecv, ratio, xin,
    g1, g0, sibs, sibr, own, gys, gyr, pad, canvas, posr, gps, h1, h, h2, k2, k3, load,
    w_ss, w_rs, rl_ss, rl_rs, p_ss, p_rs, a_ss, a_rs, ah_ss, ah_rs, pw_ss, pw_rs,
    sb_ss, sb_rs, gy_ss, gy_rs, ps_ss, ps_rs, f1_ss, f1_rs, f2_ss, f2_rs, f3_ss, f3_rs,
    *, n_pos,
):
    p = lax.axis_index("pos")
    t = lax.axis_index("tile")
    y = lax.div(t, 2)
    c = lax.rem(t, 2)
    S = ker.shape[1]
    H = S // 2
    layers, _, SR, C = strip.shape
    CW = C // n_pos
    slots = amp.shape[0]
    groups = counts.shape[0]
    RW = SR * 2 * LINE
    PR = S // n_pos
    N = math.isqrt(n_pos)
    at_axis = (lax.div(p, N), lax.rem(p, N))

    def axis_dev(n, d):
        x, z = at_axis
        if n == 0:
            return (lax.rem(x + d, N) * N + z, t)
        return (x * N + lax.rem(z + d, N), t)

    def at_y(i):
        return lax.rem(y + i, LINE)

    def ydev(i):
        return (p, 2 * at_y(i) + c)

    sib = (p, 2 * y + 1 - c)

    def pdev(d):
        return (lax.rem(p + d, n_pos), t)

    def copy(src, dst, ss, rs, dev):
        return pltpu.make_async_remote_copy(
            src_ref=src, dst_ref=dst, send_sem=ss, recv_sem=rs, device_id=dev, device_id_type=MESH
        )

    ins = (strip_in, probe_in, amp_in, amat_in, bmat_in, ker_in)
    held = (strip, probe, amp, amat, bmat, ker)
    loads = [pltpu.make_async_copy(ins[n], held[n], load.at[n]) for n in range(len(ins))]
    for one in loads:
        one.start()

    barrier = pltpu.get_barrier_semaphore()
    partners = [ydev(i) for i in range(1, LINE)] + [sib] + [pdev(d) for d in range(1, n_pos)]
    for dev in partners:
        pl.semaphore_signal(barrier, inc=1, device_id=dev, device_id_type=MESH)

    def locate(k):
        g = jnp.int32(0)
        start = jnp.int32(0)
        end = jnp.int32(0)
        for q in range(groups):
            end = end + counts[q]
            past = end <= k
            g = jnp.where(past, q + 1, g)
            start = jnp.where(past, end, start)
        return jnp.clip(slots * g + (k - start), 0, slots * groups - 1)

    row_of, base_of, shift_of = [], [], []
    for i in range(LINE):
        s = locate(LINE * p + at_y(i))
        row_of.append(offs[0, s])
        col = offs[1, s]
        block = jnp.int32(0)
        for q in range(1, (C - S) // 128):
            block = jnp.where(col >= q * 128, q, block)
        base_of.append(block)
        shift_of.append(col - block * 128)
    wide = S + 128
    my_row = row_of[0]

    my_start = jnp.int32(0)
    for q in range(groups):
        my_start = my_start + jnp.where(q < p, counts[q], 0)
    my_count = counts[p]

    def crop(l):
        for q in range(C // 128):
            tall[l, q] = strip[l, :, :, q * 128 : (q + 1) * 128].reshape(2 * SR, 128)
        for i in range(LINE):
            sel = one_hot((wide, S), shift_of[i])
            blk = jnp.concatenate([tall[l, base_of[i] + q] for q in range(wide // 128)], axis=-1)
            out = dot(blk, sel).astype(BF16).reshape(2, SR, S)
            if i == 0:
                wbuf[l, :, pl.ds(pl.multiple_of(t * SR, SR), SR), :] = out
            else:
                wsend[l, i] = out

    def strip_rows(i):
        return pl.ds(pl.multiple_of((2 * at_y(i) + c) * SR, SR), SR)

    def w_copy(l, i):
        mine = pl.ds(pl.multiple_of(t * SR, SR), SR)
        return copy(wsend.at[l, i], wbuf.at[l, :, mine, :], w_ss.at[l, i], w_rs.at[l, i], ydev(i))

    def relay(l, i):
        ref = wbuf.at[l, :, strip_rows(LINE - i), :]
        return copy(ref, ref, rl_ss.at[l, i], rl_rs.at[l, i], sib)

    def p_copy(i):
        return copy(prb.at[0], prb.at[i], p_ss.at[i], p_rs.at[i], ydev(LINE - i))

    def p_pass(n):
        i = (1, 3)[n]
        return copy(prb.at[i, n], prb.at[2, n], p_ss.at[2 * n], p_rs.at[2 * n], ydev(LINE - i))

    def a_copy(d):
        return copy(asend.at[d], arecv.at[d], a_ss.at[d], a_rs.at[d], pdev(d))

    near = (1, 3, 2)
    loads[0].wait()
    crop(0)
    loads[1].wait()
    prb[0] = probe[0].astype(BF16)
    pl.semaphore_wait(barrier, len(partners))
    for i in near:
        w_copy(0, i).start()
    relay(0, 0).start()
    crop(1)
    for i in near:
        w_copy(1, i).start()
    for i in (1, 3):
        p_copy(i).start()
    relay(1, 0).start()

    loads[2].wait()
    rows_c = pl.ds(pl.multiple_of(c * H, H), H)
    for d in range(n_pos):
        j = LINE * lax.rem(p + d, n_pos) + y - my_start
        keep = jnp.where((j >= 0) & (j < my_count), 1.0, 0.0)
        block = amp[jnp.clip(j, 0, slots - 1), rows_c, :].astype(F32) * keep
        if d == 0:
            arecv[0] = block.astype(BF16)
        else:
            asend[d] = block.astype(BF16)
    for d in range(1, n_pos):
        a_copy(d).start()

    def gather(l):
        for i in near:
            w_copy(l, i).wait_recv()
            relay(l, i).start()
        for i in range(LINE):
            relay(l, i).wait_recv()
        sel = one_hot((S, RW), my_row, transposed=True)
        win[l, 0] = dot(sel, wbuf[l, 0])
        win[l, 1] = dot(sel, wbuf[l, 1])

    def transform(re, im, left, right):
        x = jnp.concatenate([re.astype(BF16), im.astype(BF16)], axis=0)
        return transform_low(x, left, right)

    def transform_low(x, left, right):
        mid = dot(left[...], x).astype(BF16)
        out = dot(jnp.concatenate([mid[:S], mid[S:]], axis=1), right[...])
        return out[:, :S], out[:, S:]

    def forward_a(i):
        pr, pi = prb[i, 0].astype(F32), prb[i, 1].astype(F32)
        wr, wi = win[0, 0], win[0, 1]
        fr, fi = transform(pr * wr - pi * wi, pr * wi + pi * wr, amat, bmat)
        kr, ki = ker[0], ker[1]
        fr, fi = transform(fr * kr - fi * ki, fr * ki + fi * kr, bmat, amat)
        phi[i, 0] = fr
        phi[i, 1] = fi

    def forward_b(i):
        pr, pi = phi[i, 0], phi[i, 1]
        wr, wi = win[1, 0], win[1, 1]
        fr, fi = transform(pr * wr - pi * wi, pr * wi + pi * wr, amat, bmat)
        far[i, 0] = fr
        far[i, 1] = fi
        return fr * fr + fi * fi

    for l in range(layers):
        for i in range(LINE):
            for part in range(2):
                pad[l, part, i, 0] = jnp.zeros((SR, 128), BF16)
                pad[l, part, i, wide // 128 + 1] = jnp.zeros((SR, 128), BF16)
    gather(0)
    for n in (3, 4, 5):
        loads[n].wait()
    forward_a(0)
    gather(1)
    ratio[...] = forward_b(0)
    for n in range(2):
        p_copy((1, 3)[n]).wait_recv()
        p_pass(n).start()
    for i in near:
        if i == 2:
            p_pass(0).wait_recv()
            p_pass(1).wait_recv()
        forward_a(i)
        ratio[...] = ratio[...] + forward_b(i)

    pw_c = copy(pwsend, pwrecv, pw_ss.at[0], pw_rs.at[0], sib)
    pwsend[...] = ratio[...].astype(BF16)
    pw_c.start()
    total = arecv[0].astype(F32)
    for d in range(1, n_pos):
        a_copy(d).wait_recv()
        total = total + arecv[d].astype(F32)
    ahalf[rows_c, :] = total.astype(BF16)
    ah_c = copy(ahalf.at[rows_c, :], ahalf.at[rows_c, :], ah_ss.at[0], ah_rs.at[0], sib)
    ah_c.start()
    pw_c.wait_recv()
    power = ratio[...] + pwrecv[...].astype(F32)
    ah_c.wait_recv()
    ratio[...] = 1.0 - ahalf[...].astype(F32) / jnp.sqrt(power + 1.0)

    def backward_a(i, first):
        r = ratio[...]
        br, bi = transform(r * far[i, 0], r * far[i, 1], bmat, amat)
        pr, pi = phi[i, 0], phi[i, 1]
        gr = pr * br + pi * bi
        gi = pr * bi - pi * br
        if first:
            g1[0] = gr
            g1[1] = gi
        else:
            g1[0] = g1[0] + gr
            g1[1] = g1[1] + gi
        wr, wi = win[1, 0], win[1, 1]
        xin[i, :S] = (wr * br + wi * bi).astype(BF16)
        xin[i, S:] = (wr * bi - wi * br).astype(BF16)

    def backward_b(i, first):
        fr, fi = transform_low(xin[i], amat, bmat)
        kr, ki = ker[0], ker[1]
        br, bi = transform(fr * kr + fi * ki, fi * kr - fr * ki, bmat, amat)
        pr, pi = prb[i, 0].astype(F32), prb[i, 1].astype(F32)
        gr = pr * br + pi * bi
        gi = pr * bi - pi * br
        if first:
            g0[0] = gr
            g0[1] = gi
        else:
            g0[0] = g0[0] + gr
            g0[1] = g0[1] + gi
        wr, wi = win[0, 0], win[0, 1]
        pr = (wr * br + wi * bi).astype(BF16)
        pi = (wr * bi - wi * br).astype(BF16)
        for a in range(N):
            for b in range(N):
                rows = slice((a * N + b) * PR, (a * N + b + 1) * PR)
                gps[i, 0, a, b] = pr[rows]
                gps[i, 1, b, a] = pi[rows]

    def sb_copy(l, m):
        return copy(sibs.at[l, m], sibr.at[l, m], sb_ss.at[l, m], sb_rs.at[l, m], sib)

    def gy_copy(l, m, i):
        return copy(gys.at[l, m, i], gyr.at[l, m, i], gy_ss.at[l, m, i], gy_rs.at[l, m, i], ydev(i))

    def ps_copy(l, m, d):
        src = canvas.at[l, m, lax.rem(p + d, n_pos)]
        return copy(src, posr.at[l, m, d], ps_ss.at[l, m, d], ps_rs.at[l, m, d], pdev(d))

    def place_rows(l, grad):
        rows = lax.broadcasted_iota(jnp.int32, (RW, S), 0)
        cols = lax.broadcasted_iota(jnp.int32, (RW, S), 1)
        block = rows // SR
        strip_at = 2 * ((y + block % LINE) % LINE) + jnp.where(block < LINE, c, 1 - c)
        hit = strip_at * SR + rows % SR == cols + my_row
        sel = jnp.where(hit, 1.0, 0.0).astype(BF16)
        for m in range(2):
            out = dot(sel, grad[m].astype(BF16)).astype(BF16)
            for i in range(LINE):
                own[l, m, i] = out[i * SR : (i + 1) * SR]
                sibs[l, m, i] = out[(LINE + i) * SR : (LINE + i + 1) * SR]
            sb_copy(l, m).start()

    def add_cores(l, m):
        sb_copy(l, m).wait_recv()
        for i in (2, 1, 3, 0):
            both = (own[l, m, i].astype(F32) + sibr[l, m, i].astype(F32)).astype(BF16)
            if i == 0:
                gyr[l, m, 0] = both
            else:
                gys[l, m, i] = both
                gy_copy(l, m, i).start()

    def place_columns(l, m):
        for i in (0, 1, 3, 2):
            if i:
                gy_copy(l, m, i).wait_recv()
            k = (LINE - i) % LINE
            sel = one_hot((S, wide), shift_of[k], transposed=True)
            out = dot(gyr[l, m, i], sel).astype(BF16)
            for q in range(wide // 128):
                pad[l, m, i, q + 1] = out[:, q * 128 : (q + 1) * 128]
        per = CW // 128
        for q in range(C // 128):
            total = None
            for i in range(LINE):
                k = (LINE - i) % LINE
                at = jnp.clip(q - base_of[k], -1, wide // 128) + 1
                term = pad[l, m, i, at].astype(F32)
                total = term if total is None else total + term
            canvas[l, m, q // per, :, (q % per) * 128 : (q % per + 1) * 128] = total.astype(BF16)
        for d in range(1, n_pos):
            ps_copy(l, m, d).start()

    def finish(l, m):
        total = canvas[l, m, p].astype(F32)
        for d in range(1, n_pos):
            ps_copy(l, m, d).wait_recv()
            total = total + posr[l, m, d].astype(F32)
        obj_out[l, m] = total

    def f1_copy(m, d, i):
        src = gps.at[i, m, lax.rem(at_axis[m] + d, N)]
        return copy(src, h1.at[m, d, i], f1_ss.at[m, d, i], f1_rs.at[m, d, i], axis_dev(m, d))

    def f2_copy(m, d):
        src = h.at[m, lax.rem(at_axis[1 - m] + d, N)]
        return copy(src, h2.at[m, d], f2_ss.at[m, d], f2_rs.at[m, d], axis_dev(1 - m, d))

    def f3_copy(i):
        return copy(k2.at[i], k3.at[i], f3_ss.at[i], f3_rs.at[i], ydev(i))

    def first_sum(m):
        for i in range(LINE):
            total = gps[i, m, at_axis[m]].astype(F32)
            for d in range(1, N):
                f1_copy(m, d, i).wait_recv()
                total = total + h1[m, d, i].astype(F32)
            for b in range(N):
                h[m, b, i] = total[b].astype(BF16)
        for d in range(1, N):
            f2_copy(m, d).start()

    def second_sum(m):
        total = h[m, at_axis[1 - m]].astype(F32)
        for d in range(1, N):
            f2_copy(m, d).wait_recv()
            total = total + h2[m, d].astype(F32)
        for i in range(LINE):
            k2[i, m] = total[i].astype(BF16)

    for n, i in enumerate((2, 1, 3, 0)):
        backward_a(i, n == 0)
    place_rows(1, g1)
    for n, i in enumerate((2, 1, 3, 0)):
        backward_b(i, n == 0)
        for d in range(1, N):
            for m in range(2):
                f1_copy(m, d, i).start()
        if n == 0:
            add_cores(1, 0)
            add_cores(1, 1)
        if n == 2:
            place_columns(1, 0)
            place_columns(1, 1)
    place_rows(0, g0)
    add_cores(0, 0)
    add_cores(0, 1)
    first_sum(0)
    first_sum(1)
    place_columns(0, 0)
    place_columns(0, 1)
    second_sum(0)
    second_sum(1)
    for i in range(1, LINE):
        f3_copy(i).start()
    finish(1, 0)
    finish(1, 1)
    total = k2[0].astype(F32)
    for i in range(1, LINE):
        f3_copy(i).wait_recv()
        total = total + k3[i].astype(F32)
    prb_out[0] = total
    finish(0, 0)
    finish(0, 1)

    for i in (1, 3):
        p_copy(i).wait_send()
    for i in range(1, LINE):
        f3_copy(i).wait_send()
        for l in range(layers):
            w_copy(l, i).wait_send()
            for m in range(2):
                gy_copy(l, m, i).wait_send()
    for l in range(layers):
        for i in range(LINE):
            relay(l, i).wait_send()
        for m in range(2):
            sb_copy(l, m).wait_send()
            for d in range(1, n_pos):
                ps_copy(l, m, d).wait_send()
    for d in range(1, n_pos):
        a_copy(d).wait_send()
    for m in range(2):
        p_pass(m).wait_send()
        for d in range(1, N):
            f2_copy(m, d).wait_send()
            for i in range(LINE):
                f1_copy(m, d, i).wait_send()
    pw_c.wait_send()
    ah_c.wait_send()


def on_device(n_pos, consts, probe_modes, object_slices, amplitudes, scan_offsets, slot_counts):
    S = probe_modes.shape[-1]
    layers, _, SR, C = object_slices.shape
    CW = C // n_pos
    RW = SR * 2 * LINE
    wide = S + 128
    vm = pltpu.VMEM
    dma = pltpu.SemaphoreType.DMA
    PR = S // n_pos
    N = math.isqrt(n_pos)
    scratch = [
        vm(probe_modes.shape, F32),
        vm(object_slices.shape, BF16),
        vm(amplitudes.shape, BF16),
        vm((2 * S, 2 * S), BF16),
        vm((2 * S, 2 * S), BF16),
        vm((2, S, S), F32),
        vm((layers, C // 128, 2 * SR, 128), BF16),
        vm((layers, LINE, 2, SR, S), BF16),
        vm((layers, 2, RW, S), BF16),
        vm((layers, 2, S, S), F32),
        vm((LINE, 2, S, S), BF16),
        vm((n_pos, S // 2, S), BF16),
        vm((n_pos, S // 2, S), BF16),
        vm((S, S), BF16),
        vm((LINE, 2, S, S), F32),
        vm((LINE, 2, S, S), F32),
        vm((S, S), BF16),
        vm((S, S), BF16),
        vm((S, S), F32),
        vm((LINE, 2 * S, S), BF16),
        vm((2, S, S), F32),
        vm((2, S, S), F32),
        vm((layers, 2, LINE, SR, S), BF16),
        vm((layers, 2, LINE, SR, S), BF16),
        vm((layers, 2, LINE, SR, S), BF16),
        vm((layers, 2, LINE, SR, S), BF16),
        vm((layers, 2, LINE, SR, S), BF16),
        vm((layers, 2, LINE, wide // 128 + 2, SR, 128), BF16),
        vm((layers, 2, n_pos, SR, CW), BF16),
        vm((layers, 2, n_pos, SR, CW), BF16),
        vm((LINE, 2, N, N, PR, S), BF16),
        vm((2, N, LINE, N, PR, S), BF16),
        vm((2, N, LINE, PR, S), BF16),
        vm((2, N, LINE, PR, S), BF16),
        vm((LINE, 2, PR, S), BF16),
        vm((LINE, 2, PR, S), BF16),
        dma((6,)),
    ]
    for shape in (
        (layers, LINE), (layers, LINE), (LINE,), (n_pos,), (1,), (1,),
        (layers, 2), (layers, 2, LINE), (layers, 2, n_pos), (2, N, LINE), (2, N), (LINE,),
    ):
        scratch += [dma(shape), dma(shape)]
    smem = pl.BlockSpec(memory_space=pltpu.SMEM)
    vmem = pl.BlockSpec(memory_space=pltpu.VMEM)
    return pl.pallas_call(
        functools.partial(body, n_pos=n_pos),
        out_shape=(
            jax.ShapeDtypeStruct((layers, 2, SR, CW), F32),
            jax.ShapeDtypeStruct((1, 2, S // n_pos, S), F32),
        ),
        in_specs=[smem, smem] + [pl.BlockSpec(memory_space=pltpu.HBM)] * 6,
        out_specs=(vmem, vmem),
        scratch_shapes=scratch,
        compiler_params=pltpu.CompilerParams(
            collective_id=0, has_side_effects=True, vmem_limit_bytes=60 * 1024 * 1024
        ),
        name="ptycho",
    )(slot_counts, scan_offsets.T, probe_modes, object_slices, amplitudes, *consts)


def solution(mesh):
    n_pos = mesh.shape["pos"]
    in_specs = (
        P("tile", None, None, None),
        P(None, None, "tile", None),
        P("pos", None, None),
        P(),
        P(),
    )
    out_specs = (P(None, None, "tile", "pos"), P("tile", None, "pos", None))

    def run(probe_modes, object_slices, amplitudes, scan_offsets, slot_counts):
        consts = tuple(jnp.asarray(v) for v in tables(probe_modes.shape[-1]))
        return jax.shard_map(
            lambda *args: on_device(n_pos, args[5:], *args[:5]),
            mesh=mesh,
            in_specs=in_specs + (P(), P(), P()),
            out_specs=out_specs,
            check_vma=False,
        )(probe_modes, object_slices, amplitudes, scan_offsets, slot_counts, *consts)

    return run
```
